128 devices in a mesh: req: 16 (over z, x), exp: 8 (over y, core).
Axes of the slice: x: 4, y: 4, z: 4, core: 2. Of those that a mesh axis runs over, the one named last changes fastest.
Arguments:
- hidden: bfloat16 [16384, 2048], P(('req', 'exp')), may hold values from -6 to 6
- queries: bfloat16 [16384, 3072], P(('req', 'exp')), may hold values from -8 to 8
- suffix_latent: bfloat16 [16384, 576], P(('req', 'exp')), may hold values from -6 to 6
- prefix_latent: bfloat16 [16384, 576], P(('req', 'exp')), may hold values from -8 to 8
- uk_weight: bfloat16 [16, 128, 512], replicated, may hold values from -0.5 to 0.5
- uv_weight: bfloat16 [16, 512, 128], replicated, may hold values from -3 to 3
- out_weight: bfloat16 [2048, 2048], replicated, may hold values from -0.125 to 0.125
- norm_gain: float32 [2048], replicated, may hold values from 0.1 to 1.9
- expert_gate: bfloat16 [128, 2048, 704], P(('req', 'exp')), may hold values from -0.125 to 0.125
- expert_up: bfloat16 [128, 2048, 704], P(('req', 'exp')), may hold values from -0.125 to 0.125
- expert_down: bfloat16 [128, 704, 2048], P(('req', 'exp')), may hold values from -0.15625 to 0.15625
- suffix_lengths: int32 [16, 4], P('req'), may hold values from 1 to 512, 1024 in all within a row
- prefix_ids: int32 [16, 1], P('req'), may hold values from 0 to 7
- prefix_owner: int32 [16], replicated, may hold values from 0 to 15, each once
- expert_ids: int32 [16384, 6], P(('req', 'exp')), may hold values from 0 to 63, all different within a row; in each aligned block of 128 rows (0 to 127, 128 to 255, ...) at most 14 rows name the same one
- gate_weights: float32 [16384, 6], P(('req', 'exp')), may hold values from 0.1 to 0.8
Outputs:
- attended: bfloat16 [16384, 2048], P(('req', 'exp'))
- layer_out: bfloat16 [16384, 2048], P(('req', 'exp'))
The draws below stay inside these ranges and needn't reach their ends.
Inputs may be any that keep to these rules, and one draw needn't show every extreme that they name: `suffix_lengths`: each group's 4 lengths sum to 1024. `prefix_ids`: every prefix is read by some request group. `prefix_owner`: all entries differ. `expert_ids`: a token names 6 different experts; among the 128 tokens of one device no expert is named more than 14 times.
All inputs are finite; a program needn't handle non-finite values.
Results may differ from the reference program's by a relative error of at most 0.012.
Values may be sent and summed in bfloat16 or wider, within the bound.
A program may use at most 192 MiB of HBM per device.

```python
import math
import jax
import jax.numpy as jnp
import numpy as np
from jax import lax

D = 2048
HEADS = 16
NOPE = 128
ROPE = 64
V_DIM = 128
KV_RANK = 512
EXPERTS = 64
FF = 1408
TOPK = 6
TOK_DEV = 128
REQ_ROW = 4
PLEN = 1024
CAP = 14
GRP_TOK = 1024
TOKENS = 16384
PREFIXES = 8
SLOTS = 16
N_REQ = 16
N_EXP = 8


def draw_queries(key, part):
    base_key = jax.random.fold_in(key, 11)
    values = jnp.clip(jax.random.normal(base_key, (TOKENS, HEADS, NOPE + ROPE), jnp.float32), -6.0, 6.0)
    return values.reshape(TOKENS, HEADS * (NOPE + ROPE)).astype(jnp.bfloat16)


def draw_prefix_latent(key, part):
    row_count = SLOTS * PLEN
    base_key = jax.random.fold_in(key, 23)
    values = jnp.clip(jax.random.normal(base_key, (row_count, KV_RANK + ROPE), jnp.float32), -6.0, 6.0)
    return values.astype(jnp.bfloat16)


def block_levels(stream_key, extent, shards, smallest, high):
    def one(dim, shards_of):
        draws = jax.random.uniform(jax.random.fold_in(jax.random.fold_in(stream_key, 6), dim), (shards_of,), jnp.float32, smallest / len(shards), high / len(shards))
        return jnp.repeat(jnp.exp(draws), extent[dim] // shards_of).reshape((-1,) + (1,) * (len(extent) - dim - 1))

    factor_of = one(*shards[0])
    for cut in shards[1:]:
        factor_of = factor_of * one(*cut)
    return factor_of


def picks_of(rng, rows, amount, top, lift):
    order = jax.random.permutation(jax.random.fold_in(rng, 1), amount)
    boost = order
    for power in range(3):
        boost = boost * boost // amount
    boost = boost * lift // amount
    chance = jax.random.randint(jax.random.fold_in(rng, 2), (rows, amount), 0, 4096) + boost
    fixed_rows = jax.random.permutation(jax.random.fold_in(rng, 3), rows)[jnp.arange(amount) % rows]
    chance = jnp.where(jnp.arange(rows)[:, None] == fixed_rows[None, :], 1 << 14, chance)
    priority = chance * amount + jnp.arange(amount)
    return lax.top_k(priority.astype(jnp.int32), top)[1].astype(jnp.int32)


def split_up(amount, total, limit, slope):
    portions = [(1 << 20) // math.isqrt(standing ** slope) + 1 for standing in range(2, amount + 1)]
    surplus, holding = total - limit - (amount - 1), [1] * (amount - 1)
    while surplus > 0:
        free = [i for i in range(amount - 1) if holding[i] < limit]
        mass, remaining = sum([portions[i] for i in free]), surplus
        for i in free:
            extra = min(limit - holding[i], max(1, remaining * portions[i] // mass), surplus)
            holding[i] = holding[i] + extra
            surplus = surplus - extra
    return np.array([limit] + holding)


def uneven(stream_key, number_of, total, bound, skew):
    if number_of == 2:
        one = jax.random.randint(stream_key, (), max(1, total - bound), min(bound, total - 1) + 1)
        return jnp.stack([one, total - one])
    sizes = jnp.asarray(split_up(number_of, total, bound, skew), jnp.int32)
    pairs = (number_of - 1) // 2
    giver, taker = sizes[1:1 + 2 * pairs:2], sizes[2:2 + 2 * pairs:2]
    room = jnp.minimum(giver - 1, bound - taker)
    shifted = jax.random.randint(jax.random.fold_in(stream_key, 1), (pairs,), 0, 1 << 20) % (room + 1)
    sizes = sizes.at[1:1 + 2 * pairs:2].set(giver - shifted).at[2:2 + 2 * pairs:2].set(taker + shifted)
    return sizes[jax.random.permutation(jax.random.fold_in(stream_key, 2), number_of)]


def deal_out(key, own, number, rows, amount, top, limit, slope):
    order = jax.random.permutation(key, amount)
    heavy_load, ordinary = shares(amount, rows * top, limit, slope, True), shares(amount, rows * top, limit, slope, False)
    places = jnp.arange(amount)

    def named(sizes, offset_by):
        used = int((sizes > 0).sum())
        fixed = max(1, used // 4)
        passed = fixed + (places - fixed + offset_by * (used - fixed)) % max(1, amount - fixed)
        return jnp.zeros((amount,), jnp.int32).at[order[jnp.where(places < fixed, places, passed)]].set(jnp.asarray(sizes, jnp.int32))

    sizes = jnp.where(number % 4 == 0, named(heavy_load, number // 4), named(ordinary, number - number // 4 - 1))
    mixed = jax.random.permutation(jax.random.fold_in(own, 3), amount)
    giver, taker = mixed[0:amount // 2 * 2:2], mixed[1:amount // 2 * 2:2]
    slack = jnp.minimum(sizes[giver] - 1, limit - sizes[taker]) // 2
    slack = jnp.where((giver == order[0]) | (taker == order[0]) | (sizes[taker] == 0), 0, jnp.maximum(slack, 0))
    passed = jax.random.randint(jax.random.fold_in(own, 4), (amount // 2,), 0, 1 << 20) % (slack + 1)
    sizes = sizes.at[giver].add(-passed).at[taker].add(passed)
    members = jnp.searchsorted(jnp.cumsum(sizes), jnp.arange(rows * top), side="right").astype(jnp.int32)
    table = members.reshape(top, rows).T
    table = table[jax.random.permutation(jax.random.fold_in(own, 1), rows)]
    offset_by = jax.random.randint(jax.random.fold_in(own, 2), (rows, 1), 0, top)
    return jnp.take_along_axis(table, (jnp.arange(top)[None, :] + offset_by) % top, axis=1)


def shares(count, total, limit, slope, full):
    weights = [(1 << 20) // math.isqrt(rank ** slope) + 1 for rank in range(1, count + 1)]
    largest = limit if full else min(limit, max(-(-total // count), total * weights[0] // sum(weights)))
    least = 1 if total - largest >= count - 1 else 0
    given, spare = [largest] + [least] * (count - 1), total - largest - least * (count - 1)
    while spare > 0:
        free = [i for i in range(1, count) if given[i] < largest] or [i for i in range(1, count) if given[i] < limit]
        whole, left = sum([weights[i] for i in free]), spare
        for i in free:
            more = min(limit - given[i], max(1, left * weights[i] // whole), spare)
            given[i] = given[i] + more
            spare = spare - more
    return np.array(given)


def normal_values(own_key, shape, deviation, bound, cuts=(), kind=jnp.bfloat16):
    entries = deviation * jax.random.normal(own_key, shape, jnp.float32)
    if cuts:
        entries = entries * block_levels(own_key, shape, cuts, -0.22, 0.18)
    return jnp.clip(entries, -bound, bound).astype(kind)


def setup_inputs(seed: int = 0) -> dict:
    splits = jax.random.split(jax.random.key(seed), 17)
    hidden = normal_values(splits[0], (TOKENS, D), 1.0, 6.0, ((0, 128),))
    queries = draw_queries(jax.random.fold_in(splits[16], 71), 0)
    suffix_latent = normal_values(splits[2], (TOKENS, KV_RANK + ROPE), 1.0, 6.0, ((0, 128),))
    prefix_latent = draw_prefix_latent(jax.random.fold_in(splits[16], 71), 0)
    uk_weight = normal_values(splits[4], (HEADS, NOPE, KV_RANK), NOPE ** -0.5, 0.5)
    uv_weight = normal_values(splits[5], (HEADS, KV_RANK, V_DIM), (max(KV_RANK // 128, 1)) ** -0.5, 3.0)
    out_weight = normal_values(splits[6], (HEADS * V_DIM, D), (HEADS * V_DIM) ** -0.5, 0.125)
    norm_gain = jnp.clip(1.0 + 0.18 * jax.random.normal(splits[7], (D,), jnp.float32), 0.1, 1.9)
    expert_gate = normal_values(splits[8], (2 * EXPERTS, D, FF // 2), D ** -0.5, 0.125, ((0, 128),))
    expert_up = normal_values(splits[9], (2 * EXPERTS, D, FF // 2), D ** -0.5, 0.125, ((0, 128),))
    expert_down = normal_values(splits[10], (2 * EXPERTS, FF // 2, D), FF ** -0.5, 0.15625, ((0, 128),))
    suffix_lengths = jax.vmap(lambda own: uneven(own, REQ_ROW, GRP_TOK, GRP_TOK // 2, 2))(jax.random.split(splits[11], N_REQ)).reshape((N_REQ, REQ_ROW)).astype(jnp.int32)
    prefix_ids = picks_of(splits[12], N_REQ, PREFIXES, 1, 2048)
    prefix_owner = jax.random.permutation(splits[13], SLOTS).astype(jnp.int32)
    expert_ids_keys = jax.random.split(jax.random.fold_in(splits[14], 1), TOKENS // TOK_DEV)
    expert_ids_turns = jax.random.permutation(jax.random.fold_in(splits[14], 3), TOKENS // TOK_DEV)
    expert_ids = jax.vmap(lambda own, number: deal_out(jax.random.fold_in(splits[14], 2), own, number, TOK_DEV, EXPERTS, TOPK, CAP, 2))(expert_ids_keys, expert_ids_turns).reshape((TOKENS, TOPK))
    gate_weights = jnp.clip(0.1 + 0.7 * jax.random.uniform(splits[15], (TOKENS, TOPK), jnp.float32) ** block_levels(splits[15], (TOKENS, TOPK), ((0, 128),), -0.2, 0.2), 0.1, 0.8)
    return {"hidden": hidden, "queries": queries, "suffix_latent": suffix_latent, "prefix_latent": prefix_latent, "uk_weight": uk_weight, "uv_weight": uv_weight, "out_weight": out_weight, "norm_gain": norm_gain, "expert_gate": expert_gate, "expert_up": expert_up, "expert_down": expert_down, "suffix_lengths": suffix_lengths, "prefix_ids": prefix_ids, "prefix_owner": prefix_owner, "expert_ids": expert_ids, "gate_weights": gate_weights}


masked_score = -1e+30

def request_of(positions, lengths):
    request_ends = jnp.cumsum(lengths)
    return lax.optimization_barrier(jnp.sum((positions[:, None] >= request_ends[None, :]).astype(jnp.int32), axis=1))

def reference(hidden, queries, suffix_latent, prefix_latent, uk_weight, uv_weight, out_weight, norm_gain, expert_gate, expert_up, expert_down, suffix_lengths, prefix_ids, prefix_owner, expert_ids, gate_weights):
    score_scale = (NOPE + ROPE) ** (-0.5)
    q_split = queries.reshape(TOKENS, HEADS, NOPE + ROPE)

    def group_block(flat_index):
        group_index = flat_index // N_EXP
        block_index = flat_index % N_EXP
        first_row = (group_index * GRP_TOK + block_index * TOK_DEV).astype(jnp.int32)
        q_rows = lax.dynamic_slice_in_dim(q_split, first_row, TOK_DEV, 0)
        q_latent = jnp.einsum('thn,hnc->thc', q_rows[:, :, :NOPE].astype(jnp.float32), uk_weight.astype(jnp.float32)).astype(jnp.bfloat16)
        q_abs = jnp.concatenate([q_latent, q_rows[:, :, NOPE:]], axis=2)
        my_slot = prefix_owner[prefix_ids[group_index, 0]]
        prefix_rows = lax.dynamic_slice_in_dim(prefix_latent, (my_slot * PLEN).astype(jnp.int32), PLEN, 0)
        suffix_rows = lax.dynamic_slice_in_dim(suffix_latent, (group_index * GRP_TOK).astype(jnp.int32), GRP_TOK, 0)
        key_rows = jnp.concatenate([prefix_rows, suffix_rows], axis=0)
        lengths = suffix_lengths[group_index]
        q_pos = block_index * TOK_DEV + jnp.arange(TOK_DEV, dtype=jnp.int32)
        k_pos = jnp.arange(GRP_TOK, dtype=jnp.int32)
        same_request = request_of(q_pos, lengths)[:, None] == request_of(k_pos, lengths)[None, :]
        causal = k_pos[None, :] <= q_pos[:, None]
        visible = jnp.concatenate([jnp.ones((TOK_DEV, PLEN), jnp.bool_), same_request & causal], axis=1)
        scores = jnp.einsum('thc,nc->thn', q_abs.astype(jnp.float32), key_rows.astype(jnp.float32)) * score_scale
        scores = jnp.where(visible[:, None, :], scores, masked_score)
        top_score = lax.optimization_barrier(jnp.max(scores, axis=2, keepdims=True))
        prob_terms = jnp.where(visible[:, None, :], jnp.exp(scores - top_score), 0.0)
        weight_sum = lax.optimization_barrier(jnp.sum(prob_terms, axis=2))
        weights = prob_terms.astype(jnp.bfloat16)
        latent_acc = jnp.einsum('thn,nc->thc', weights.astype(jnp.float32), key_rows[:, :KV_RANK].astype(jnp.float32))
        latent_out = (latent_acc / weight_sum[:, :, None]).astype(jnp.bfloat16)
        heads_out = jnp.einsum('thc,hcv->thv', latent_out.astype(jnp.float32), uv_weight.astype(jnp.float32)).astype(jnp.bfloat16)
        heads_out = heads_out.reshape(TOK_DEV, HEADS * V_DIM)
        return jnp.dot(heads_out, out_weight, preferred_element_type=jnp.float32).astype(jnp.bfloat16)
    attended = lax.map(group_block, jnp.arange(N_REQ * N_EXP, dtype=jnp.int32)).reshape(TOKENS, D)
    residual = hidden.astype(jnp.float32) + attended.astype(jnp.float32)
    mean_square = lax.optimization_barrier(jnp.mean(residual * residual, axis=1, keepdims=True))
    normed = (residual * lax.rsqrt(mean_square + 1e-06) * norm_gain).astype(jnp.bfloat16)
    max_rows = N_REQ * N_EXP * CAP

    def one_expert(routed_sum, expert_index):
        hit = expert_ids == expert_index
        picked = jnp.any(hit, axis=1)
        pick_weight = lax.optimization_barrier(jnp.sum(jnp.where(hit, gate_weights, 0.0), axis=1))
        row_ids = jnp.nonzero(picked, size=max_rows, fill_value=0)[0].astype(jnp.int32)
        valid = jnp.arange(max_rows, dtype=jnp.int32) < jnp.sum(picked.astype(jnp.int32))
        chosen = normed[row_ids].astype(jnp.float32)
        both_parts = jnp.zeros((max_rows, D), jnp.float32)
        for half_index in range(2):
            half_expert = 2 * expert_index + half_index
            gate_proj = chosen @ expert_gate[half_expert].astype(jnp.float32)
            up_proj = chosen @ expert_up[half_expert].astype(jnp.float32)
            active = (jax.nn.silu(gate_proj) * up_proj).astype(jnp.bfloat16)
            part_out = (active.astype(jnp.float32) @ expert_down[half_expert].astype(jnp.float32)).astype(jnp.bfloat16)
            part_out = lax.optimization_barrier(part_out)
            both_parts = both_parts + part_out.astype(jnp.float32)
        expert_out = lax.optimization_barrier(both_parts.astype(jnp.bfloat16)).astype(jnp.float32)
        scaled = jnp.where(valid[:, None], pick_weight[row_ids][:, None] * expert_out, 0.0)
        return (routed_sum.at[row_ids].add(scaled), None)
    routed_sum, unused = lax.scan(one_expert, jnp.zeros((TOKENS, D), jnp.float32), jnp.arange(EXPERTS, dtype=jnp.int32))
    layer_out = (residual + routed_sum).astype(jnp.bfloat16)
    return (attended, layer_out)
```

```python
import jax
import jax.numpy as jnp
from jax import lax
from jax.sharding import Mesh, PartitionSpec as P

EXPERTS = 64
CAP = 14


masked_score = -1e30


def request_of(positions, lengths):
    request_ends = jnp.cumsum(lengths)
    return jnp.sum((positions[:, None] >= request_ends[None, :]).astype(jnp.int32), axis=1)


def per_device(
    hidden,
    queries,
    suffix_latent,
    prefix_latent,
    uk_weight,
    uv_weight,
    out_weight,
    norm_gain,
    expert_gate,
    expert_up,
    expert_down,
    suffix_lengths,
    prefix_ids,
    prefix_owner,
    expert_ids,
    gate_weights,
):
    tok_rows = hidden.shape[0]
    head_count = uk_weight.shape[0]
    nope_width = uk_weight.shape[1]
    kv_rank = uk_weight.shape[2]
    latent_width = suffix_latent.shape[1]
    rope_width = queries.shape[1] // head_count - nope_width
    score_scale = (nope_width + rope_width) ** (-0.5)
    column = lax.axis_index("y") * lax.axis_size("core") + lax.axis_index("core")
    positions = column * tok_rows + jnp.arange(tok_rows, dtype=jnp.int32)
    lengths = suffix_lengths[0]
    own_request = request_of(positions, lengths)
    my_slot = prefix_owner[prefix_ids[0, 0]]
    q_split = queries.reshape(tok_rows, head_count, nope_width + rope_width)
    q_latent = jnp.einsum(
        "thn,hnc->thc", q_split[:, :, :nope_width], uk_weight, preferred_element_type=jnp.float32
    ).astype(jnp.bfloat16)
    q_abs = jnp.concatenate([q_latent, q_split[:, :, nope_width:]], axis=2)
    slot_chunks = lax.all_gather(prefix_latent, "req", axis=0, tiled=False)
    my_chunk = lax.dynamic_index_in_dim(slot_chunks, my_slot, 0, keepdims=False)
    both = jnp.concatenate([my_chunk, suffix_latent], axis=1)
    gathered = lax.all_gather(both, ("y", "core"), axis=0, tiled=True)
    prefix_rows = gathered[:, :latent_width]
    suffix_rows = gathered[:, latent_width:]
    key_rows = jnp.concatenate([prefix_rows, suffix_rows], axis=0)
    key_pos = jnp.arange(suffix_rows.shape[0], dtype=jnp.int32)
    key_request = request_of(key_pos, lengths)
    visible_suffix = (key_request[None, :] == own_request[:, None]) & (
        key_pos[None, :] <= positions[:, None]
    )
    visible = jnp.concatenate(
        [jnp.ones((tok_rows, prefix_rows.shape[0]), jnp.bool_), visible_suffix], axis=1
    )
    scores = (
        jnp.einsum("thc,nc->thn", q_abs, key_rows, preferred_element_type=jnp.float32) * score_scale
    )
    scores = jnp.where(visible[:, None, :], scores, masked_score)
    top_score = jnp.max(scores, axis=2, keepdims=True)
    prob_terms = jnp.where(visible[:, None, :], jnp.exp(scores - top_score), 0.0)
    weight_sum = jnp.sum(prob_terms, axis=2)
    latent_acc = jnp.einsum(
        "thn,nc->thc",
        prob_terms.astype(jnp.bfloat16),
        key_rows[:, :kv_rank],
        preferred_element_type=jnp.float32,
    )
    latent_out = (latent_acc / weight_sum[:, :, None]).astype(jnp.bfloat16)
    heads_out = jnp.einsum(
        "thc,hcv->thv", latent_out, uv_weight, preferred_element_type=jnp.float32
    ).astype(jnp.bfloat16)
    heads_out = heads_out.reshape(tok_rows, -1)
    attended = jnp.dot(heads_out, out_weight, preferred_element_type=jnp.float32).astype(
        jnp.bfloat16
    )
    residual = hidden.astype(jnp.float32) + attended.astype(jnp.float32)
    mean_square = jnp.mean(residual * residual, axis=1, keepdims=True)
    normed = (residual * lax.rsqrt(mean_square + 1e-06) * norm_gain).astype(jnp.bfloat16)
    experts = EXPERTS
    capacity = CAP
    top_picks = expert_ids.shape[1]
    flat_ids = expert_ids.reshape(-1)
    onehot = (flat_ids[:, None] == jnp.arange(experts, dtype=jnp.int32)[None, :]).astype(jnp.int32)
    slot_rank = jnp.sum((jnp.cumsum(onehot, axis=0) - 1) * onehot, axis=1)
    target = flat_ids * capacity + slot_rank
    placing = (jnp.arange(experts * capacity, dtype=jnp.int32)[:, None] == target[None, :]).astype(
        jnp.bfloat16
    )
    placing = placing.reshape(experts * capacity, tok_rows, top_picks).sum(axis=2)
    packed_rows = jnp.dot(placing, normed, preferred_element_type=jnp.float32).astype(jnp.bfloat16)
    width = packed_rows.shape[1]
    packed = packed_rows.reshape(experts, capacity, width)
    recv_rows = lax.all_to_all(packed, ("req", "y"), 0, 0, tiled=True)
    chip_rows = lax.all_gather(recv_rows, "core", axis=0, tiled=False)
    chip_rows = chip_rows.reshape(-1, width)
    gate_proj = jnp.dot(chip_rows, expert_gate[0], preferred_element_type=jnp.float32)
    up_proj = jnp.dot(chip_rows, expert_up[0], preferred_element_type=jnp.float32)
    active = (jax.nn.silu(gate_proj) * up_proj).astype(jnp.bfloat16)
    part = jnp.dot(active, expert_down[0], preferred_element_type=jnp.float32).astype(jnp.bfloat16)
    core_count = lax.axis_size("core")
    part = part.reshape(core_count, -1, width)
    both_parts = lax.all_to_all(part, "core", 0, 0, tiled=True)
    pair_total = jnp.sum(both_parts.astype(jnp.float32), axis=0).astype(jnp.bfloat16)
    returned = lax.all_to_all(
        pair_total.reshape(experts, capacity, width), ("req", "y"), 0, 0, tiled=True
    )
    summed = returned.reshape(experts * capacity, width).astype(jnp.float32)
    picked_rows = jnp.take(summed, target, axis=0).reshape(tok_rows, top_picks, width)
    routed = jnp.sum(gate_weights[:, :, None] * picked_rows, axis=1)
    layer_out = (residual + routed).astype(jnp.bfloat16)
    return (attended, layer_out)


def solution(mesh):
    req_count = mesh.shape["req"]
    exp_count = mesh.shape["exp"]
    chip_mesh = Mesh(
        mesh.devices.reshape(req_count, exp_count // 2, 2), ("req", "y", "core")
    )
    rows = ("req", "y", "core")
    in_specs = (
        P(rows, None),
        P(rows, None),
        P(rows, None),
        P(rows, None),
        P(),
        P(),
        P(),
        P(),
        P(rows, None, None),
        P(rows, None, None),
        P(rows, None, None),
        P("req", None),
        P("req", None),
        P(),
        P(rows, None),
        P(rows, None),
    )
    out_specs = (P(rows, None), P(rows, None))
    return jax.shard_map(
        per_device, mesh=chip_mesh, in_specs=in_specs, out_specs=out_specs, check_vma=False
    )
```

```python
import jax
import jax.numpy as jnp
from jax import lax
from jax.sharding import Mesh, PartitionSpec as P

EXPERTS = 64
CAP = 14


masked_score = -1e30


def request_of(positions, lengths):
    request_ends = jnp.cumsum(lengths)
    return jnp.sum((positions[:, None] >= request_ends[None, :]).astype(jnp.int32), axis=1)


def per_device(
    hidden,
    queries,
    suffix_latent,
    prefix_latent,
    uk_weight,
    uv_weight,
    out_weight,
    norm_gain,
    expert_gate,
    expert_up,
    expert_down,
    suffix_lengths,
    prefix_ids,
    prefix_owner,
    expert_ids,
    gate_weights,
):
    tok_rows = hidden.shape[0]
    head_count = uk_weight.shape[0]
    nope_width = uk_weight.shape[1]
    kv_rank = uk_weight.shape[2]
    latent_width = suffix_latent.shape[1]
    rope_width = queries.shape[1] // head_count - nope_width
    score_scale = (nope_width + rope_width) ** (-0.5)
    column = lax.axis_index("y") * lax.axis_size("core") + lax.axis_index("core")
    positions = column * tok_rows + jnp.arange(tok_rows, dtype=jnp.int32)
    lengths = suffix_lengths[0]
    own_request = request_of(positions, lengths)
    my_slot = prefix_owner[prefix_ids[0, 0]]
    q_split = queries.reshape(tok_rows, head_count, nope_width + rope_width)
    q_latent = jnp.einsum(
        "thn,hnc->thc", q_split[:, :, :nope_width], uk_weight, preferred_element_type=jnp.float32
    ).astype(jnp.bfloat16)
    q_abs = jnp.concatenate([q_latent, q_split[:, :, nope_width:]], axis=2)
    slot_chunks = lax.all_gather(prefix_latent, "req", axis=0, tiled=False)
    my_chunk = lax.dynamic_index_in_dim(slot_chunks, my_slot, 0, keepdims=False)
    both = jnp.concatenate([my_chunk, suffix_latent], axis=1)
    gathered = lax.all_gather(both, ("y", "core"), axis=0, tiled=True)
    prefix_rows = gathered[:, :latent_width]
    suffix_rows = gathered[:, latent_width:]
    key_rows = jnp.concatenate([prefix_rows, suffix_rows], axis=0)
    key_pos = jnp.arange(suffix_rows.shape[0], dtype=jnp.int32)
    key_request = request_of(key_pos, lengths)
    visible_suffix = (key_request[None, :] == own_request[:, None]) & (
        key_pos[None, :] <= positions[:, None]
    )
    visible = jnp.concatenate(
        [jnp.ones((tok_rows, prefix_rows.shape[0]), jnp.bool_), visible_suffix], axis=1
    )
    scores = (
        jnp.einsum("thc,nc->thn", q_abs, key_rows, preferred_element_type=jnp.float32) * score_scale
    )
    scores = jnp.where(visible[:, None, :], scores, masked_score)
    top_score = jnp.max(scores, axis=2, keepdims=True)
    prob_terms = jnp.where(visible[:, None, :], jnp.exp(scores - top_score), 0.0)
    weight_sum = jnp.sum(prob_terms, axis=2)
    latent_acc = jnp.einsum(
        "thn,nc->thc",
        prob_terms.astype(jnp.bfloat16),
        key_rows[:, :kv_rank],
        preferred_element_type=jnp.float32,
    )
    latent_out = (latent_acc / weight_sum[:, :, None]).astype(jnp.bfloat16)
    heads_out = jnp.einsum(
        "thc,hcv->thv", latent_out, uv_weight, preferred_element_type=jnp.float32
    ).astype(jnp.bfloat16)
    heads_out = heads_out.reshape(tok_rows, -1)
    attended = jnp.dot(heads_out, out_weight, preferred_element_type=jnp.float32).astype(
        jnp.bfloat16
    )
    residual = hidden.astype(jnp.float32) + attended.astype(jnp.float32)
    mean_square = jnp.mean(residual * residual, axis=1, keepdims=True)
    normed = (residual * lax.rsqrt(mean_square + 1e-06) * norm_gain).astype(jnp.bfloat16)
    experts = EXPERTS
    capacity = -(-CAP // 16) * 16
    top_picks = expert_ids.shape[1]
    slots = experts * capacity
    flat_ids = expert_ids.reshape(-1)
    onehot = (flat_ids[:, None] == jnp.arange(experts, dtype=jnp.int32)[None, :]).astype(jnp.int32)
    slot_rank = jnp.sum((jnp.cumsum(onehot, axis=0) - 1) * onehot, axis=1)
    target = flat_ids * capacity + slot_rank
    hits = jnp.arange(slots, dtype=jnp.int32)[None, :] == target[:, None]
    placing = hits.astype(jnp.bfloat16).reshape(tok_rows, top_picks, slots).sum(axis=1)
    packed = lax.dot_general(
        placing, normed, (((0,), (0,)), ((), ())), preferred_element_type=jnp.float32
    ).astype(jnp.bfloat16)
    width = packed.shape[1]
    recv_rows = lax.all_to_all(packed, ("req", "y"), 0, 0, tiled=True)
    chip_rows = lax.all_gather(recv_rows, "core", axis=0, tiled=True)
    gate_proj = jnp.dot(chip_rows, expert_gate[0], preferred_element_type=jnp.float32)
    up_proj = jnp.dot(chip_rows, expert_up[0], preferred_element_type=jnp.float32)
    active = (jax.nn.silu(gate_proj) * up_proj).astype(jnp.bfloat16)
    part = jnp.dot(active, expert_down[0], preferred_element_type=jnp.float32).astype(jnp.bfloat16)
    both_parts = lax.all_to_all(part, "core", 0, 0, tiled=True)
    pair_total = (
        both_parts[:slots].astype(jnp.float32) + both_parts[slots:].astype(jnp.float32)
    ).astype(jnp.bfloat16)
    returned = lax.all_to_all(pair_total, ("req", "y"), 0, 0, tiled=True)
    pick_weight = jnp.sum(
        jnp.where(hits.reshape(tok_rows, top_picks, slots), gate_weights[:, :, None], 0.0), axis=1
    )
    routed = jnp.dot(
        pick_weight,
        returned.astype(jnp.float32),
        precision=lax.Precision.HIGHEST,
        preferred_element_type=jnp.float32,
    )
    layer_out = (residual + routed).astype(jnp.bfloat16)
    return (attended, layer_out)


def solution(mesh):
    req_count = mesh.shape["req"]
    exp_count = mesh.shape["exp"]
    chip_mesh = Mesh(
        mesh.devices.reshape(req_count, exp_count // 2, 2), ("req", "y", "core")
    )
    rows = ("req", "y", "core")
    in_specs = (
        P(rows, None),
        P(rows, None),
        P(rows, None),
        P(rows, None),
        P(),
        P(),
        P(),
        P(),
        P(rows, None, None),
        P(rows, None, None),
        P(rows, None, None),
        P("req", None),
        P("req", None),
        P(),
        P(rows, None),
        P(rows, None),
    )
    out_specs = (P(rows, None), P(rows, None))
    return jax.shard_map(
        per_device, mesh=chip_mesh, in_specs=in_specs, out_specs=out_specs, check_vma=False
    )
```

```python
import jax
import jax.numpy as jnp
from jax import lax
from jax.sharding import Mesh, PartitionSpec as P

EXPERTS = 64
CAP = 14


masked_score = -1e30


def request_of(positions, lengths):
    request_ends = jnp.cumsum(lengths)
    return jnp.sum((positions[:, None] >= request_ends[None, :]).astype(jnp.int32), axis=1)


def layer(
    hidden,
    queries,
    suffix_latent,
    prefix_latent,
    uk_weight,
    uv_weight,
    out_weight,
    norm_gain,
    expert_gate,
    expert_up,
    expert_down,
    suffix_lengths,
    prefix_ids,
    prefix_owner,
    expert_ids,
    gate_weights,
):
    tok_rows = hidden.shape[0]
    head_count = uk_weight.shape[0]
    nope_width = uk_weight.shape[1]
    kv_rank = uk_weight.shape[2]
    latent_width = suffix_latent.shape[1]
    rope_width = queries.shape[1] // head_count - nope_width
    score_scale = (nope_width + rope_width) ** (-0.5)
    column = lax.axis_index("y") * lax.axis_size("core") + lax.axis_index("core")
    positions = column * tok_rows + jnp.arange(tok_rows, dtype=jnp.int32)
    lengths = suffix_lengths[0]
    own_request = request_of(positions, lengths)
    my_slot = prefix_owner[prefix_ids[0, 0]]
    q_split = queries.reshape(tok_rows, head_count, nope_width + rope_width)
    q_latent = jnp.einsum(
        "thn,hnc->thc", q_split[:, :, :nope_width], uk_weight, preferred_element_type=jnp.float32
    ).astype(jnp.bfloat16)
    q_abs = jnp.concatenate([q_latent, q_split[:, :, nope_width:]], axis=2)
    slot_chunks = lax.all_gather(prefix_latent, "req", axis=0, tiled=False)
    my_chunk = lax.dynamic_index_in_dim(slot_chunks, my_slot, 0, keepdims=False)
    both = jnp.concatenate([my_chunk, suffix_latent], axis=1)
    gathered = lax.all_gather(both, ("y", "core"), axis=0, tiled=True)
    prefix_rows = gathered[:, :latent_width]
    suffix_rows = gathered[:, latent_width:]
    key_rows = jnp.concatenate([prefix_rows, suffix_rows], axis=0)
    key_pos = jnp.arange(suffix_rows.shape[0], dtype=jnp.int32)
    key_request = request_of(key_pos, lengths)
    visible_suffix = (key_request[None, :] == own_request[:, None]) & (
        key_pos[None, :] <= positions[:, None]
    )
    visible = jnp.concatenate(
        [jnp.ones((tok_rows, prefix_rows.shape[0]), jnp.bool_), visible_suffix], axis=1
    )
    scores = (
        jnp.einsum("thc,nc->thn", q_abs, key_rows, preferred_element_type=jnp.float32)
        * score_scale
    )
    scores = jnp.where(visible[:, None, :], scores, masked_score)
    top_score = jnp.max(scores, axis=2, keepdims=True)
    prob_terms = jnp.where(visible[:, None, :], jnp.exp(scores - top_score), 0.0)
    weight_sum = jnp.sum(prob_terms, axis=2)
    latent_acc = jnp.einsum(
        "thn,nc->thc",
        prob_terms.astype(jnp.bfloat16),
        key_rows[:, :kv_rank],
        preferred_element_type=jnp.float32,
    )
    latent_out = (latent_acc / weight_sum[:, :, None]).astype(jnp.bfloat16)
    heads_out = jnp.einsum(
        "thc,hcv->thv", latent_out, uv_weight, preferred_element_type=jnp.float32
    ).astype(jnp.bfloat16)
    heads_out = heads_out.reshape(tok_rows, -1)
    attended = jnp.dot(heads_out, out_weight, preferred_element_type=jnp.float32).astype(
        jnp.bfloat16
    )
    residual = hidden.astype(jnp.float32) + attended.astype(jnp.float32)
    mean_square = jnp.mean(residual * residual, axis=1, keepdims=True)
    normed = (residual * lax.rsqrt(mean_square + 1e-06) * norm_gain).astype(jnp.bfloat16)
    experts = EXPERTS
    capacity = -(-CAP // 16) * 16
    top_picks = expert_ids.shape[1]
    slots = experts * capacity
    flat_ids = expert_ids.reshape(-1)
    onehot = (flat_ids[:, None] == jnp.arange(experts, dtype=jnp.int32)[None, :]).astype(jnp.int32)
    slot_rank = jnp.sum((jnp.cumsum(onehot, axis=0) - 1) * onehot, axis=1)
    target = flat_ids * capacity + slot_rank
    hits = jnp.arange(slots, dtype=jnp.int32)[None, :] == target[:, None]
    placing = hits.astype(jnp.bfloat16).reshape(tok_rows, top_picks, slots).sum(axis=1)
    packed = lax.dot_general(
        placing, normed, (((0,), (0,)), ((), ())), preferred_element_type=jnp.float32
    ).astype(jnp.bfloat16)
    swap = [(0, 1), (1, 0)]
    sibling_gate = lax.ppermute(expert_gate, "core", swap)
    sibling_up = lax.ppermute(expert_up, "core", swap)
    sibling_down = lax.ppermute(expert_down, "core", swap)
    recv_rows = lax.all_to_all(packed, ("req", "y"), 0, 0, tiled=True)

    def half_expert(gate_w, up_w, down_w):
        gate_proj = jnp.dot(recv_rows, gate_w, preferred_element_type=jnp.float32)
        up_proj = jnp.dot(recv_rows, up_w, preferred_element_type=jnp.float32)
        active = (jax.nn.silu(gate_proj) * up_proj).astype(jnp.bfloat16)
        return jnp.dot(active, down_w, preferred_element_type=jnp.float32).astype(jnp.bfloat16)

    own_part = half_expert(expert_gate[0], expert_up[0], expert_down[0])
    sibling_part = half_expert(sibling_gate[0], sibling_up[0], sibling_down[0])
    pair_total = (own_part.astype(jnp.float32) + sibling_part.astype(jnp.float32)).astype(
        jnp.bfloat16
    )
    returned = lax.all_to_all(pair_total, ("req", "y"), 0, 0, tiled=True)
    pick_weight = jnp.sum(
        jnp.where(hits.reshape(tok_rows, top_picks, slots), gate_weights[:, :, None], 0.0), axis=1
    )
    routed = jnp.dot(
        pick_weight,
        returned.astype(jnp.float32),
        precision=lax.Precision.HIGHEST,
        preferred_element_type=jnp.float32,
    )
    layer_out = (residual + routed).astype(jnp.bfloat16)
    return (attended, layer_out)


def solution(mesh):
    req_count = mesh.shape["req"]
    exp_count = mesh.shape["exp"]
    chip_mesh = Mesh(
        mesh.devices.reshape(req_count, exp_count // 2, 2), ("req", "y", "core")
    )
    rows = ("req", "y", "core")
    in_specs = (
        P(rows, None),
        P(rows, None),
        P(rows, None),
        P(rows, None),
        P(),
        P(),
        P(),
        P(),
        P(rows, None, None),
        P(rows, None, None),
        P(rows, None, None),
        P("req", None),
        P("req", None),
        P(),
        P(rows, None),
        P(rows, None),
    )
    out_specs = (P(rows, None), P(rows, None))
    return jax.shard_map(
        layer, mesh=chip_mesh, in_specs=in_specs, out_specs=out_specs, check_vma=False
    )
```

```python
import jax
import jax.numpy as jnp
from jax import lax
from jax.sharding import Mesh, PartitionSpec as P

EXPERTS = 64
CAP = 14


masked_score = -1e30


def request_of(positions, lengths):
    request_ends = jnp.cumsum(lengths)
    return jnp.sum((positions[:, None] >= request_ends[None, :]).astype(jnp.int32), axis=1)


def layer(
    hidden,
    queries,
    suffix_latent,
    prefix_latent,
    uk_weight,
    uv_weight,
    out_weight,
    norm_gain,
    expert_gate,
    expert_up,
    expert_down,
    suffix_lengths,
    prefix_ids,
    prefix_owner,
    expert_ids,
    gate_weights,
):
    tok_rows = hidden.shape[0]
    head_count = uk_weight.shape[0]
    nope_width = uk_weight.shape[1]
    kv_rank = uk_weight.shape[2]
    latent_width = suffix_latent.shape[1]
    rope_width = queries.shape[1] // head_count - nope_width
    score_scale = (nope_width + rope_width) ** (-0.5)
    column = lax.axis_index("y") * lax.axis_size("core") + lax.axis_index("core")
    positions = column * tok_rows + jnp.arange(tok_rows, dtype=jnp.int32)
    lengths = suffix_lengths[0]
    own_request = request_of(positions, lengths)
    my_group = lax.axis_index("z") * lax.axis_size("x") + lax.axis_index("x")
    my_slot = prefix_owner[prefix_ids[my_group, 0]]
    q_split = queries.reshape(tok_rows, head_count, nope_width + rope_width)
    q_latent = jnp.einsum(
        "thn,hnc->thc", q_split[:, :, :nope_width], uk_weight, preferred_element_type=jnp.float32
    ).astype(jnp.bfloat16)
    q_abs = jnp.concatenate([q_latent, q_split[:, :, nope_width:]], axis=2)
    x_count = lax.axis_size("x")
    z_count = lax.axis_size("z")
    my_x = lax.axis_index("x")
    group_slots = prefix_owner[prefix_ids[:, 0]]
    x_chunks = lax.all_gather(prefix_latent, "x", axis=0, tiled=False)
    dest_slots = group_slots.reshape(z_count, x_count)[:, my_x]
    sent = jnp.take(x_chunks, dest_slots % x_count, axis=0)
    recv_chunks = lax.all_to_all(sent, "z", 0, 0, tiled=True)
    my_chunk = lax.dynamic_index_in_dim(recv_chunks, my_slot // x_count, 0, keepdims=False)
    both = jnp.concatenate([my_chunk, suffix_latent], axis=1)
    gathered = lax.all_gather(both, ("y", "core"), axis=0, tiled=True)
    prefix_rows = gathered[:, :latent_width]
    suffix_rows = gathered[:, latent_width:]
    key_rows = jnp.concatenate([prefix_rows, suffix_rows], axis=0)
    key_pos = jnp.arange(suffix_rows.shape[0], dtype=jnp.int32)
    key_request = request_of(key_pos, lengths)
    visible_suffix = (key_request[None, :] == own_request[:, None]) & (
        key_pos[None, :] <= positions[:, None]
    )
    visible = jnp.concatenate(
        [jnp.ones((tok_rows, prefix_rows.shape[0]), jnp.bool_), visible_suffix], axis=1
    )
    scores = (
        jnp.einsum("thc,nc->thn", q_abs, key_rows, preferred_element_type=jnp.float32)
        * score_scale
    )
    scores = jnp.where(visible[:, None, :], scores, masked_score)
    top_score = jnp.max(scores, axis=2, keepdims=True)
    prob_terms = jnp.where(visible[:, None, :], jnp.exp(scores - top_score), 0.0)
    weight_sum = jnp.sum(prob_terms, axis=2)
    latent_acc = jnp.einsum(
        "thn,nc->thc",
        prob_terms.astype(jnp.bfloat16),
        key_rows[:, :kv_rank],
        preferred_element_type=jnp.float32,
    )
    latent_out = (latent_acc / weight_sum[:, :, None]).astype(jnp.bfloat16)
    heads_out = jnp.einsum(
        "thc,hcv->thv", latent_out, uv_weight, preferred_element_type=jnp.float32
    ).astype(jnp.bfloat16)
    heads_out = heads_out.reshape(tok_rows, -1)
    attended = jnp.dot(heads_out, out_weight, preferred_element_type=jnp.float32).astype(
        jnp.bfloat16
    )
    residual = hidden.astype(jnp.float32) + attended.astype(jnp.float32)
    mean_square = jnp.mean(residual * residual, axis=1, keepdims=True)
    normed = (residual * lax.rsqrt(mean_square + 1e-06) * norm_gain).astype(jnp.bfloat16)
    experts = EXPERTS
    capacity = -(-CAP // 16) * 16
    top_picks = expert_ids.shape[1]
    slots = experts * capacity
    flat_ids = expert_ids.reshape(-1)
    onehot = (flat_ids[:, None] == jnp.arange(experts, dtype=jnp.int32)[None, :]).astype(jnp.int32)
    slot_rank = jnp.sum((jnp.cumsum(onehot, axis=0) - 1) * onehot, axis=1)
    target = flat_ids * capacity + slot_rank
    hits = jnp.arange(slots, dtype=jnp.int32)[None, :] == target[:, None]
    placing = hits.astype(jnp.bfloat16).reshape(tok_rows, top_picks, slots).sum(axis=1)
    packed = lax.dot_general(
        placing, normed, (((0,), (0,)), ((), ())), preferred_element_type=jnp.float32
    ).astype(jnp.bfloat16)
    swap = [(0, 1), (1, 0)]
    sibling_gate = lax.ppermute(expert_gate, "core", swap)
    sibling_up = lax.ppermute(expert_up, "core", swap)
    sibling_down = lax.ppermute(expert_down, "core", swap)
    recv_rows = lax.all_to_all(packed, ("z", "x", "y"), 0, 0, tiled=True)

    def half_expert(gate_w, up_w, down_w):
        gate_proj = jnp.dot(recv_rows, gate_w, preferred_element_type=jnp.float32)
        up_proj = jnp.dot(recv_rows, up_w, preferred_element_type=jnp.float32)
        active = (jax.nn.silu(gate_proj) * up_proj).astype(jnp.bfloat16)
        return jnp.dot(active, down_w, preferred_element_type=jnp.float32).astype(jnp.bfloat16)

    own_part = half_expert(expert_gate[0], expert_up[0], expert_down[0])
    sibling_part = half_expert(sibling_gate[0], sibling_up[0], sibling_down[0])
    pair_total = (own_part.astype(jnp.float32) + sibling_part.astype(jnp.float32)).astype(
        jnp.bfloat16
    )
    returned = lax.all_to_all(pair_total, ("z", "x", "y"), 0, 0, tiled=True)
    pick_weight = jnp.sum(
        jnp.where(hits.reshape(tok_rows, top_picks, slots), gate_weights[:, :, None], 0.0), axis=1
    )
    routed = jnp.dot(
        pick_weight,
        returned.astype(jnp.float32),
        precision=lax.Precision.HIGHEST,
        preferred_element_type=jnp.float32,
    )
    layer_out = (residual + routed).astype(jnp.bfloat16)
    return (attended, layer_out)


def solution(mesh):
    req_count = mesh.shape["req"]
    exp_count = mesh.shape["exp"]
    x_count = 4
    chip_mesh = Mesh(
        mesh.devices.reshape(req_count // x_count, x_count, exp_count // 2, 2),
        ("z", "x", "y", "core"),
    )
    rows = ("z", "x", "y", "core")
    groups = ("z", "x")
    in_specs = (
        P(rows, None),
        P(rows, None),
        P(rows, None),
        P(rows, None),
        P(),
        P(),
        P(),
        P(),
        P(rows, None, None),
        P(rows, None, None),
        P(rows, None, None),
        P(groups, None),
        P(),
        P(),
        P(rows, None),
        P(rows, None),
    )
    out_specs = (P(rows, None), P(rows, None))
    return jax.shard_map(
        layer, mesh=chip_mesh, in_specs=in_specs, out_specs=out_specs, check_vma=False
    )
```

```python
import jax
import jax.numpy as jnp
from jax import lax
from jax.sharding import Mesh, PartitionSpec as P

EXPERTS = 64
CAP = 14


masked_score = -1e30


def request_of(positions, lengths):
    request_ends = jnp.cumsum(lengths)
    return jnp.sum((positions[:, None] >= request_ends[None, :]).astype(jnp.int32), axis=1)


def layer(
    hidden,
    queries,
    suffix_latent,
    prefix_latent,
    uk_weight,
    uv_weight,
    out_weight,
    norm_gain,
    expert_gate,
    expert_up,
    expert_down,
    suffix_lengths,
    prefix_ids,
    prefix_owner,
    expert_ids,
    gate_weights,
):
    tok_rows = hidden.shape[0]
    head_count = uk_weight.shape[0]
    nope_width = uk_weight.shape[1]
    kv_rank = uk_weight.shape[2]
    rope_width = queries.shape[1] // head_count - nope_width
    score_scale = (nope_width + rope_width) ** (-0.5)
    column = lax.axis_index("y") * lax.axis_size("core") + lax.axis_index("core")
    positions = column * tok_rows + jnp.arange(tok_rows, dtype=jnp.int32)
    lengths = suffix_lengths[0]
    own_request = request_of(positions, lengths)
    my_slot = prefix_owner[prefix_ids[0, 0]]
    q_split = queries.reshape(tok_rows, head_count, nope_width + rope_width)
    q_latent = jnp.einsum(
        "thn,hnc->thc", q_split[:, :, :nope_width], uk_weight, preferred_element_type=jnp.float32
    ).astype(jnp.bfloat16)
    q_abs = jnp.concatenate([q_latent, q_split[:, :, nope_width:]], axis=2)
    x_count = lax.axis_size("x")
    suffix_rows = lax.all_gather(suffix_latent, ("y", "core"), axis=0, tiled=True)
    dest_slots = lax.all_gather(my_slot[None], "z", axis=0, tiled=True)
    x_chunks = lax.all_gather(prefix_latent, "x", axis=0, tiled=False)
    sent = jnp.take(x_chunks, dest_slots % x_count, axis=0)
    recv_chunks = lax.all_to_all(sent, "z", 0, 0, tiled=True)
    my_chunk = lax.dynamic_index_in_dim(recv_chunks, my_slot // x_count, 0, keepdims=False)
    prefix_rows = lax.all_gather(my_chunk, ("y", "core"), axis=0, tiled=True)
    key_rows = jnp.concatenate([prefix_rows, suffix_rows], axis=0)
    key_pos = jnp.arange(suffix_rows.shape[0], dtype=jnp.int32)
    key_request = request_of(key_pos, lengths)
    visible_suffix = (key_request[None, :] == own_request[:, None]) & (
        key_pos[None, :] <= positions[:, None]
    )
    visible = jnp.concatenate(
        [jnp.ones((tok_rows, prefix_rows.shape[0]), jnp.bool_), visible_suffix], axis=1
    )
    scores = (
        jnp.einsum("thc,nc->thn", q_abs, key_rows, preferred_element_type=jnp.float32)
        * score_scale
    )
    scores = jnp.where(visible[:, None, :], scores, masked_score)
    top_score = jnp.max(scores, axis=2, keepdims=True)
    prob_terms = jnp.where(visible[:, None, :], jnp.exp(scores - top_score), 0.0)
    weight_sum = jnp.sum(prob_terms, axis=2)
    latent_acc = jnp.einsum(
        "thn,nc->thc",
        prob_terms.astype(jnp.bfloat16),
        key_rows[:, :kv_rank],
        preferred_element_type=jnp.float32,
    )
    latent_out = (latent_acc / weight_sum[:, :, None]).astype(jnp.bfloat16)
    heads_out = jnp.einsum(
        "thc,hcv->thv", latent_out, uv_weight, preferred_element_type=jnp.float32
    ).astype(jnp.bfloat16)
    heads_out = heads_out.reshape(tok_rows, -1)
    attended = jnp.dot(heads_out, out_weight, preferred_element_type=jnp.float32).astype(
        jnp.bfloat16
    )
    residual = hidden.astype(jnp.float32) + attended.astype(jnp.float32)
    mean_square = jnp.mean(residual * residual, axis=1, keepdims=True)
    normed = (residual * lax.rsqrt(mean_square + 1e-06) * norm_gain).astype(jnp.bfloat16)
    experts = EXPERTS
    capacity = -(-CAP // 16) * 16
    top_picks = expert_ids.shape[1]
    slots = experts * capacity
    flat_ids = expert_ids.reshape(-1)
    onehot = (flat_ids[:, None] == jnp.arange(experts, dtype=jnp.int32)[None, :]).astype(jnp.int32)
    slot_rank = jnp.sum((jnp.cumsum(onehot, axis=0) - 1) * onehot, axis=1)
    target = flat_ids * capacity + slot_rank
    hits = jnp.arange(slots, dtype=jnp.int32)[None, :] == target[:, None]
    placing = hits.astype(jnp.bfloat16).reshape(tok_rows, top_picks, slots).sum(axis=1)
    packed = lax.dot_general(
        placing, normed, (((0,), (0,)), ((), ())), preferred_element_type=jnp.float32
    ).astype(jnp.bfloat16)
    swap = [(0, 1), (1, 0)]
    sibling_gate = lax.ppermute(expert_gate, "core", swap)
    sibling_up = lax.ppermute(expert_up, "core", swap)
    sibling_down = lax.ppermute(expert_down, "core", swap)
    recv_rows = lax.all_to_all(packed, ("z", "x", "y"), 0, 0, tiled=True)

    def half_expert(gate_w, up_w, down_w):
        gate_proj = jnp.dot(recv_rows, gate_w, preferred_element_type=jnp.float32)
        up_proj = jnp.dot(recv_rows, up_w, preferred_element_type=jnp.float32)
        active = (jax.nn.silu(gate_proj) * up_proj).astype(jnp.bfloat16)
        return jnp.dot(active, down_w, preferred_element_type=jnp.float32).astype(jnp.bfloat16)

    own_part = half_expert(expert_gate[0], expert_up[0], expert_down[0])
    sibling_part = half_expert(sibling_gate[0], sibling_up[0], sibling_down[0])
    pair_total = (own_part.astype(jnp.float32) + sibling_part.astype(jnp.float32)).astype(
        jnp.bfloat16
    )
    returned = lax.all_to_all(pair_total, ("z", "x", "y"), 0, 0, tiled=True)
    pick_weight = jnp.sum(
        jnp.where(hits.reshape(tok_rows, top_picks, slots), gate_weights[:, :, None], 0.0), axis=1
    )
    routed = jnp.dot(
        pick_weight,
        returned.astype(jnp.float32),
        precision=lax.Precision.HIGHEST,
        preferred_element_type=jnp.float32,
    )
    layer_out = (residual + routed).astype(jnp.bfloat16)
    return (attended, layer_out)


def solution(mesh):
    req_count = mesh.shape["req"]
    exp_count = mesh.shape["exp"]
    x_count = 4
    chip_mesh = Mesh(
        mesh.devices.reshape(req_count // x_count, x_count, exp_count // 2, 2),
        ("z", "x", "y", "core"),
    )
    rows = ("z", "x", "y", "core")
    groups = ("z", "x")
    in_specs = (
        P(rows, None),
        P(rows, None),
        P(rows, None),
        P(rows, None),
        P(),
        P(),
        P(),
        P(),
        P(rows, None, None),
        P(rows, None, None),
        P(rows, None, None),
        P(groups, None),
        P(groups, None),
        P(),
        P(rows, None),
        P(rows, None),
    )
    out_specs = (P(rows, None), P(rows, None))
    return jax.shard_map(
        layer, mesh=chip_mesh, in_specs=in_specs, out_specs=out_specs, check_vma=False
    )
```

```python
import jax
import jax.numpy as jnp
from jax import lax
from jax.sharding import Mesh, PartitionSpec as P

EXPERTS = 64
CAP = 14


masked_score = -1e30


def request_of(positions, lengths):
    request_ends = jnp.cumsum(lengths)
    return jnp.sum((positions[:, None] >= request_ends[None, :]).astype(jnp.int32), axis=1)


def layer(
    hidden,
    queries,
    suffix_latent,
    prefix_latent,
    uk_weight,
    uv_weight,
    out_weight,
    norm_gain,
    expert_gate,
    expert_up,
    expert_down,
    suffix_lengths,
    prefix_ids,
    prefix_owner,
    expert_ids,
    gate_weights,
):
    tok_rows = hidden.shape[0]
    head_count = uk_weight.shape[0]
    nope_width = uk_weight.shape[1]
    kv_rank = uk_weight.shape[2]
    rope_width = queries.shape[1] // head_count - nope_width
    score_scale = (nope_width + rope_width) ** (-0.5)
    column = lax.axis_index("y") * lax.axis_size("core") + lax.axis_index("core")
    positions = column * tok_rows + jnp.arange(tok_rows, dtype=jnp.int32)
    lengths = suffix_lengths[0]
    own_request = request_of(positions, lengths)
    my_slot = prefix_owner[prefix_ids[0, 0]]
    q_split = queries.reshape(tok_rows, head_count, nope_width + rope_width)
    q_latent = jnp.einsum(
        "thn,hnc->thc", q_split[:, :, :nope_width], uk_weight, preferred_element_type=jnp.float32
    ).astype(jnp.bfloat16)
    q_abs = jnp.concatenate([q_latent, q_split[:, :, nope_width:]], axis=2)
    x_count = lax.axis_size("x")
    suffix_rows = lax.all_gather(suffix_latent, ("y", "core"), axis=0, tiled=True)
    dest_slots = lax.all_gather(my_slot[None], "z", axis=0, tiled=True)
    x_chunks = lax.all_gather(prefix_latent, "x", axis=0, tiled=False)
    sent = jnp.take(x_chunks, dest_slots % x_count, axis=0)
    recv_chunks = lax.all_to_all(sent, "z", 0, 0, tiled=True)
    my_chunk = lax.dynamic_index_in_dim(recv_chunks, my_slot // x_count, 0, keepdims=False)
    prefix_rows = lax.all_gather(my_chunk, ("y", "core"), axis=0, tiled=True)
    key_rows = jnp.concatenate([prefix_rows, suffix_rows], axis=0)
    key_pos = jnp.arange(suffix_rows.shape[0], dtype=jnp.int32)
    key_request = request_of(key_pos, lengths)
    visible_suffix = (key_request[None, :] == own_request[:, None]) & (
        key_pos[None, :] <= positions[:, None]
    )
    visible = jnp.concatenate(
        [jnp.ones((tok_rows, prefix_rows.shape[0]), jnp.bool_), visible_suffix], axis=1
    )
    scores = (
        jnp.einsum("thc,nc->thn", q_abs, key_rows, preferred_element_type=jnp.float32)
        * score_scale
    )
    scores = jnp.where(visible[:, None, :], scores, masked_score)
    top_score = jnp.max(scores, axis=2, keepdims=True)
    prob_terms = jnp.where(visible[:, None, :], jnp.exp(scores - top_score), 0.0)
    weight_sum = jnp.sum(prob_terms, axis=2)
    latent_acc = jnp.einsum(
        "thn,nc->thc",
        prob_terms.astype(jnp.bfloat16),
        key_rows[:, :kv_rank],
        preferred_element_type=jnp.float32,
    )
    latent_out = (latent_acc / weight_sum[:, :, None]).astype(jnp.bfloat16)
    heads_out = jnp.einsum(
        "thc,hcv->thv", latent_out, uv_weight, preferred_element_type=jnp.float32
    ).astype(jnp.bfloat16)
    heads_out = heads_out.reshape(tok_rows, -1)
    attended = jnp.dot(heads_out, out_weight, preferred_element_type=jnp.float32).astype(
        jnp.bfloat16
    )
    residual = hidden.astype(jnp.float32) + attended.astype(jnp.float32)
    mean_square = jnp.mean(residual * residual, axis=1, keepdims=True)
    normed = (residual * lax.rsqrt(mean_square + 1e-06) * norm_gain).astype(jnp.bfloat16)
    experts = EXPERTS
    capacity = -(-CAP // 16) * 16
    top_picks = expert_ids.shape[1]
    slots = experts * capacity
    flat_ids = expert_ids.reshape(-1)
    onehot = (flat_ids[:, None] == jnp.arange(experts, dtype=jnp.int32)[None, :]).astype(jnp.int32)
    slot_rank = jnp.sum((jnp.cumsum(onehot, axis=0) - 1) * onehot, axis=1)
    target = flat_ids * capacity + slot_rank
    hits = jnp.arange(slots, dtype=jnp.int32)[None, :] == target[:, None]
    placing = hits.astype(jnp.bfloat16).reshape(tok_rows, top_picks, slots).sum(axis=1)
    width = normed.shape[1]
    split = width // 2
    feature_halves = (slice(0, split), slice(split, width))
    swap = [(0, 1), (1, 0)]
    sibling_gate = lax.ppermute(expert_gate, "core", swap)
    sibling_up = lax.ppermute(expert_up, "core", swap)
    sibling_down = lax.ppermute(expert_down, "core", swap)
    recv_halves = []
    for cols in feature_halves:
        packed = lax.dot_general(
            placing, normed[:, cols], (((0,), (0,)), ((), ())), preferred_element_type=jnp.float32
        ).astype(jnp.bfloat16)
        recv_halves.append(lax.all_to_all(packed, ("z", "x", "y"), 0, 0, tiled=True))

    def projection(weight):
        return sum(
            jnp.dot(rows, weight[cols], preferred_element_type=jnp.float32)
            for rows, cols in zip(recv_halves, feature_halves)
        )

    def activation(gate_w, up_w):
        return (jax.nn.silu(projection(gate_w)) * projection(up_w)).astype(jnp.bfloat16)

    own_active = activation(expert_gate[0], expert_up[0])
    sibling_active = activation(sibling_gate[0], sibling_up[0])
    pick_weight = jnp.sum(
        jnp.where(hits.reshape(tok_rows, top_picks, slots), gate_weights[:, :, None], 0.0), axis=1
    )
    routed_halves = []
    for cols in feature_halves:
        own_part = jnp.dot(
            own_active, expert_down[0][:, cols], preferred_element_type=jnp.float32
        ).astype(jnp.bfloat16)
        sibling_part = jnp.dot(
            sibling_active, sibling_down[0][:, cols], preferred_element_type=jnp.float32
        ).astype(jnp.bfloat16)
        pair_total = (own_part.astype(jnp.float32) + sibling_part.astype(jnp.float32)).astype(
            jnp.bfloat16
        )
        returned = lax.all_to_all(pair_total, ("z", "x", "y"), 0, 0, tiled=True)
        routed_halves.append(
            jnp.dot(
                pick_weight,
                returned.astype(jnp.float32),
                precision=lax.Precision.HIGHEST,
                preferred_element_type=jnp.float32,
            )
        )
    routed = jnp.concatenate(routed_halves, axis=1)
    layer_out = (residual + routed).astype(jnp.bfloat16)
    return (attended, layer_out)


def solution(mesh):
    req_count = mesh.shape["req"]
    exp_count = mesh.shape["exp"]
    x_count = 4
    chip_mesh = Mesh(
        mesh.devices.reshape(req_count // x_count, x_count, exp_count // 2, 2),
        ("z", "x", "y", "core"),
    )
    rows = ("z", "x", "y", "core")
    groups = ("z", "x")
    in_specs = (
        P(rows, None),
        P(rows, None),
        P(rows, None),
        P(rows, None),
        P(),
        P(),
        P(),
        P(),
        P(rows, None, None),
        P(rows, None, None),
        P(rows, None, None),
        P(groups, None),
        P(groups, None),
        P(),
        P(rows, None),
        P(rows, None),
    )
    out_specs = (P(rows, None), P(rows, None))
    return jax.shard_map(
        layer, mesh=chip_mesh, in_specs=in_specs, out_specs=out_specs, check_vma=False
    )
```

```python
import jax
import jax.numpy as jnp
from jax import lax
from jax.sharding import Mesh, PartitionSpec as P

EXPERTS = 64
CAP = 14


masked_score = -1e30


def request_of(positions, lengths):
    request_ends = jnp.cumsum(lengths)
    return jnp.sum((positions[:, None] >= request_ends[None, :]).astype(jnp.int32), axis=1)


def layer(
    hidden,
    queries,
    suffix_latent,
    prefix_latent,
    uk_weight,
    uv_weight,
    out_weight,
    norm_gain,
    expert_gate,
    expert_up,
    expert_down,
    suffix_lengths,
    prefix_ids,
    prefix_owner,
    expert_ids,
    gate_weights,
):
    tok_rows = hidden.shape[0]
    head_count = uk_weight.shape[0]
    nope_width = uk_weight.shape[1]
    kv_rank = uk_weight.shape[2]
    rope_width = queries.shape[1] // head_count - nope_width
    score_scale = (nope_width + rope_width) ** (-0.5)
    column = lax.axis_index("y") * lax.axis_size("core") + lax.axis_index("core")
    positions = column * tok_rows + jnp.arange(tok_rows, dtype=jnp.int32)
    lengths = suffix_lengths[0]
    own_request = request_of(positions, lengths)
    my_slot = prefix_owner[prefix_ids[0, 0]]
    q_split = queries.reshape(tok_rows, head_count, nope_width + rope_width)
    q_latent = jnp.einsum(
        "thn,hnc->thc", q_split[:, :, :nope_width], uk_weight, preferred_element_type=jnp.float32
    ).astype(jnp.bfloat16)
    q_abs = jnp.concatenate([q_latent, q_split[:, :, nope_width:]], axis=2)
    x_count = lax.axis_size("x")
    z_count = lax.axis_size("z")
    suffix_rows = lax.all_gather(suffix_latent, ("y", "core"), axis=0, tiled=True)
    dest_slots = lax.all_to_all(
        jnp.broadcast_to(my_slot[None], (z_count,)), "z", 0, 0, tiled=True
    )
    x_chunks = lax.all_to_all(
        jnp.broadcast_to(prefix_latent[None], (x_count,) + prefix_latent.shape), "x", 0, 0, tiled=True
    )
    sent = jnp.take(x_chunks, dest_slots % x_count, axis=0)
    recv_chunks = lax.all_to_all(sent, "z", 0, 0, tiled=True)
    my_chunk = lax.dynamic_index_in_dim(recv_chunks, my_slot // x_count, 0, keepdims=False)
    prefix_rows = lax.all_gather(my_chunk, ("y", "core"), axis=0, tiled=True)
    key_pos = jnp.arange(suffix_rows.shape[0], dtype=jnp.int32)
    key_request = request_of(key_pos, lengths)
    visible_suffix = (key_request[None, :] == own_request[:, None]) & (
        key_pos[None, :] <= positions[:, None]
    )

    def key_scores(key_rows):
        return (
            jnp.einsum("thc,nc->thn", q_abs, key_rows, preferred_element_type=jnp.float32)
            * score_scale
        )

    def weighted_values(prob_terms, key_rows):
        return jnp.einsum(
            "thn,nc->thc",
            prob_terms.astype(jnp.bfloat16),
            key_rows[:, :kv_rank],
            preferred_element_type=jnp.float32,
        )

    suffix_scores = jnp.where(visible_suffix[:, None, :], key_scores(suffix_rows), masked_score)
    suffix_top = jnp.max(suffix_scores, axis=2)
    suffix_probs = jnp.where(
        visible_suffix[:, None, :], jnp.exp(suffix_scores - suffix_top[:, :, None]), 0.0
    )
    suffix_sum = jnp.sum(suffix_probs, axis=2)
    suffix_acc = weighted_values(suffix_probs, suffix_rows)
    prefix_scores = key_scores(prefix_rows)
    top_score = jnp.maximum(suffix_top, jnp.max(prefix_scores, axis=2))
    prefix_probs = jnp.exp(prefix_scores - top_score[:, :, None])
    factor = jnp.exp(suffix_top - top_score)
    weight_sum = suffix_sum * factor + jnp.sum(prefix_probs, axis=2)
    latent_acc = suffix_acc * factor[:, :, None] + weighted_values(prefix_probs, prefix_rows)
    latent_out = (latent_acc / weight_sum[:, :, None]).astype(jnp.bfloat16)
    heads_out = jnp.einsum(
        "thc,hcv->thv", latent_out, uv_weight, preferred_element_type=jnp.float32
    ).astype(jnp.bfloat16)
    heads_out = heads_out.reshape(tok_rows, -1)
    attended = jnp.dot(heads_out, out_weight, preferred_element_type=jnp.float32).astype(
        jnp.bfloat16
    )
    residual = hidden.astype(jnp.float32) + attended.astype(jnp.float32)
    mean_square = jnp.mean(residual * residual, axis=1, keepdims=True)
    normed = (residual * lax.rsqrt(mean_square + 1e-06) * norm_gain).astype(jnp.bfloat16)
    experts = EXPERTS
    capacity = -(-CAP // 16) * 16
    top_picks = expert_ids.shape[1]
    slots = experts * capacity
    flat_ids = expert_ids.reshape(-1)
    onehot = (flat_ids[:, None] == jnp.arange(experts, dtype=jnp.int32)[None, :]).astype(jnp.int32)
    slot_rank = jnp.sum((jnp.cumsum(onehot, axis=0) - 1) * onehot, axis=1)
    target = flat_ids * capacity + slot_rank
    hits = jnp.arange(slots, dtype=jnp.int32)[None, :] == target[:, None]
    placing = hits.astype(jnp.bfloat16).reshape(tok_rows, top_picks, slots).sum(axis=1)
    packed = lax.dot_general(
        placing, normed, (((0,), (0,)), ((), ())), preferred_element_type=jnp.float32
    ).astype(jnp.bfloat16)
    swap = [(0, 1), (1, 0)]
    sibling_gate = lax.ppermute(expert_gate, "core", swap)
    sibling_up = lax.ppermute(expert_up, "core", swap)
    sibling_down = lax.ppermute(expert_down, "core", swap)
    recv_rows = lax.all_to_all(packed, ("z", "x", "y"), 0, 0, tiled=True)

    def half_expert(gate_w, up_w, down_w):
        gate_proj = jnp.dot(recv_rows, gate_w, preferred_element_type=jnp.float32)
        up_proj = jnp.dot(recv_rows, up_w, preferred_element_type=jnp.float32)
        active = (jax.nn.silu(gate_proj) * up_proj).astype(jnp.bfloat16)
        return jnp.dot(active, down_w, preferred_element_type=jnp.float32).astype(jnp.bfloat16)

    own_part = half_expert(expert_gate[0], expert_up[0], expert_down[0])
    sibling_part = half_expert(sibling_gate[0], sibling_up[0], sibling_down[0])
    pair_total = (own_part.astype(jnp.float32) + sibling_part.astype(jnp.float32)).astype(
        jnp.bfloat16
    )
    returned = lax.all_to_all(pair_total, ("z", "x", "y"), 0, 0, tiled=True)
    pick_weight = jnp.sum(
        jnp.where(hits.reshape(tok_rows, top_picks, slots), gate_weights[:, :, None], 0.0), axis=1
    )
    routed = jnp.dot(
        pick_weight,
        returned.astype(jnp.float32),
        precision=lax.Precision.HIGHEST,
        preferred_element_type=jnp.float32,
    )
    layer_out = (residual + routed).astype(jnp.bfloat16)
    return (attended, layer_out)


def solution(mesh):
    req_count = mesh.shape["req"]
    exp_count = mesh.shape["exp"]
    x_count = 4
    chip_mesh = Mesh(
        mesh.devices.reshape(req_count // x_count, x_count, exp_count // 2, 2),
        ("z", "x", "y", "core"),
    )
    rows = ("z", "x", "y", "core")
    groups = ("z", "x")
    in_specs = (
        P(rows, None),
        P(rows, None),
        P(rows, None),
        P(rows, None),
        P(),
        P(),
        P(),
        P(),
        P(rows, None, None),
        P(rows, None, None),
        P(rows, None, None),
        P(groups, None),
        P(groups, None),
        P(),
        P(rows, None),
        P(rows, None),
    )
    out_specs = (P(rows, None), P(rows, None))
    return jax.shard_map(
        layer, mesh=chip_mesh, in_specs=in_specs, out_specs=out_specs, check_vma=False
    )
```

```python
import jax
import jax.numpy as jnp
from jax import lax
from jax.sharding import Mesh, PartitionSpec as P

EXPERTS = 64
CAP = 14


masked_score = -1e30


def request_of(positions, lengths):
    request_ends = jnp.cumsum(lengths)
    return jnp.sum((positions[:, None] >= request_ends[None, :]).astype(jnp.int32), axis=1)


def layer(
    hidden,
    queries,
    suffix_latent,
    prefix_latent,
    uk_weight,
    uv_weight,
    out_weight,
    norm_gain,
    expert_gate,
    expert_up,
    expert_down,
    suffix_lengths,
    prefix_ids,
    prefix_owner,
    expert_ids,
    gate_weights,
):
    tok_rows = hidden.shape[0]
    head_count = uk_weight.shape[0]
    nope_width = uk_weight.shape[1]
    kv_rank = uk_weight.shape[2]
    rope_width = queries.shape[1] // head_count - nope_width
    score_scale = (nope_width + rope_width) ** (-0.5)
    column = lax.axis_index("y") * lax.axis_size("core") + lax.axis_index("core")
    positions = column * tok_rows + jnp.arange(tok_rows, dtype=jnp.int32)
    lengths = suffix_lengths[0]
    own_request = request_of(positions, lengths)
    my_slot = prefix_owner[prefix_ids[0, 0]]
    q_split = queries.reshape(tok_rows, head_count, nope_width + rope_width)
    q_latent = jnp.einsum(
        "thn,hnc->thc", q_split[:, :, :nope_width], uk_weight, preferred_element_type=jnp.float32
    ).astype(jnp.bfloat16)
    q_abs = jnp.concatenate([q_latent, q_split[:, :, nope_width:]], axis=2)
    x_count = lax.axis_size("x")
    z_count = lax.axis_size("z")
    suffix_rows = lax.all_gather(suffix_latent, ("y", "core"), axis=0, tiled=True)
    dest_slots = lax.all_to_all(
        jnp.broadcast_to(my_slot[None], (z_count,)), "z", 0, 0, tiled=True
    )
    x_chunks = lax.all_to_all(
        jnp.broadcast_to(prefix_latent[None], (x_count,) + prefix_latent.shape), "x", 0, 0, tiled=True
    )
    sent = jnp.take(x_chunks, dest_slots % x_count, axis=0)
    recv_chunks = lax.all_to_all(sent, "z", 0, 0, tiled=True)
    my_chunk = lax.dynamic_index_in_dim(recv_chunks, my_slot // x_count, 0, keepdims=False)
    prefix_rows = lax.all_gather(my_chunk, ("y", "core"), axis=0, tiled=True)
    key_rows = jnp.concatenate([prefix_rows, suffix_rows], axis=0)
    key_pos = jnp.arange(suffix_rows.shape[0], dtype=jnp.int32)
    key_request = request_of(key_pos, lengths)
    visible_suffix = (key_request[None, :] == own_request[:, None]) & (
        key_pos[None, :] <= positions[:, None]
    )
    visible = jnp.concatenate(
        [jnp.ones((tok_rows, prefix_rows.shape[0]), jnp.bool_), visible_suffix], axis=1
    )
    scores = (
        jnp.einsum("thc,nc->thn", q_abs, key_rows, preferred_element_type=jnp.float32)
        * score_scale
    )
    scores = jnp.where(visible[:, None, :], scores, masked_score)
    top_score = jnp.max(scores, axis=2, keepdims=True)
    prob_terms = jnp.where(visible[:, None, :], jnp.exp(scores - top_score), 0.0)
    weight_sum = jnp.sum(prob_terms, axis=2)
    latent_acc = jnp.einsum(
        "thn,nc->thc",
        prob_terms.astype(jnp.bfloat16),
        key_rows[:, :kv_rank],
        preferred_element_type=jnp.float32,
    )
    latent_out = (latent_acc / weight_sum[:, :, None]).astype(jnp.bfloat16)
    heads_out = jnp.einsum(
        "thc,hcv->thv", latent_out, uv_weight, preferred_element_type=jnp.float32
    ).astype(jnp.bfloat16)
    heads_out = heads_out.reshape(tok_rows, -1)
    attended = jnp.dot(heads_out, out_weight, preferred_element_type=jnp.float32).astype(
        jnp.bfloat16
    )
    residual = hidden.astype(jnp.float32) + attended.astype(jnp.float32)
    mean_square = jnp.mean(residual * residual, axis=1, keepdims=True)
    normed = (residual * lax.rsqrt(mean_square + 1e-06) * norm_gain).astype(jnp.bfloat16)
    experts = EXPERTS
    capacity = -(-CAP // 16) * 16
    top_picks = expert_ids.shape[1]
    slots = experts * capacity
    flat_ids = expert_ids.reshape(-1)
    onehot = (flat_ids[:, None] == jnp.arange(experts, dtype=jnp.int32)[None, :]).astype(jnp.int32)
    slot_rank = jnp.sum((jnp.cumsum(onehot, axis=0) - 1) * onehot, axis=1)
    target = flat_ids * capacity + slot_rank
    hits = jnp.arange(slots, dtype=jnp.int32)[None, :] == target[:, None]
    placing = hits.astype(jnp.bfloat16).reshape(tok_rows, top_picks, slots).sum(axis=1)
    packed = lax.dot_general(
        placing, normed, (((0,), (0,)), ((), ())), preferred_element_type=jnp.float32
    ).astype(jnp.bfloat16)
    swap = [(0, 1), (1, 0)]
    sibling_gate = lax.ppermute(expert_gate, "core", swap)
    sibling_up = lax.ppermute(expert_up, "core", swap)
    sibling_down = lax.ppermute(expert_down, "core", swap)
    recv_rows = lax.all_to_all(packed, ("z", "x", "y"), 0, 0, tiled=True)

    def half_expert(gate_w, up_w, down_w):
        gate_proj = jnp.dot(recv_rows, gate_w, preferred_element_type=jnp.float32)
        up_proj = jnp.dot(recv_rows, up_w, preferred_element_type=jnp.float32)
        active = lax.optimization_barrier((jax.nn.silu(gate_proj) * up_proj).astype(jnp.bfloat16))
        return jnp.dot(active, down_w, preferred_element_type=jnp.float32).astype(jnp.bfloat16)

    own_part = half_expert(expert_gate[0], expert_up[0], expert_down[0])
    sibling_part = half_expert(sibling_gate[0], sibling_up[0], sibling_down[0])
    pair_total = (own_part.astype(jnp.float32) + sibling_part.astype(jnp.float32)).astype(
        jnp.bfloat16
    )
    returned = lax.all_to_all(pair_total, ("z", "x", "y"), 0, 0, tiled=True)
    pick_weight = jnp.sum(
        jnp.where(hits.reshape(tok_rows, top_picks, slots), gate_weights[:, :, None], 0.0), axis=1
    )
    routed = jnp.dot(
        pick_weight,
        returned.astype(jnp.float32),
        precision=lax.Precision.HIGHEST,
        preferred_element_type=jnp.float32,
    )
    layer_out = (residual + routed).astype(jnp.bfloat16)
    return (attended, layer_out)


def solution(mesh):
    req_count = mesh.shape["req"]
    exp_count = mesh.shape["exp"]
    x_count = 4
    chip_mesh = Mesh(
        mesh.devices.reshape(req_count // x_count, x_count, exp_count // 2, 2),
        ("z", "x", "y", "core"),
    )
    rows = ("z", "x", "y", "core")
    groups = ("z", "x")
    in_specs = (
        P(rows, None),
        P(rows, None),
        P(rows, None),
        P(rows, None),
        P(),
        P(),
        P(),
        P(),
        P(rows, None, None),
        P(rows, None, None),
        P(rows, None, None),
        P(groups, None),
        P(groups, None),
        P(),
        P(rows, None),
        P(rows, None),
    )
    out_specs = (P(rows, None), P(rows, None))
    return jax.shard_map(
        layer, mesh=chip_mesh, in_specs=in_specs, out_specs=out_specs, check_vma=False
    )
```

```python
import jax
import jax.numpy as jnp
from jax import lax
from jax.sharding import Mesh, PartitionSpec as P

EXPERTS = 64
CAP = 14


masked_score = -1e30


def request_of(positions, lengths):
    request_ends = jnp.cumsum(lengths)
    return jnp.sum((positions[:, None] >= request_ends[None, :]).astype(jnp.int32), axis=1)


def layer(
    hidden,
    queries,
    suffix_latent,
    prefix_latent,
    uk_weight,
    uv_weight,
    out_weight,
    norm_gain,
    expert_gate,
    expert_up,
    expert_down,
    suffix_lengths,
    prefix_ids,
    prefix_owner,
    expert_ids,
    gate_weights,
):
    tok_rows = hidden.shape[0]
    head_count = uk_weight.shape[0]
    nope_width = uk_weight.shape[1]
    kv_rank = uk_weight.shape[2]
    rope_width = queries.shape[1] // head_count - nope_width
    score_scale = (nope_width + rope_width) ** (-0.5)
    column = lax.axis_index("y") * lax.axis_size("core") + lax.axis_index("core")
    positions = column * tok_rows + jnp.arange(tok_rows, dtype=jnp.int32)
    lengths = suffix_lengths[0]
    own_request = request_of(positions, lengths)
    my_slot = prefix_owner[prefix_ids[0, 0]]
    q_split = queries.reshape(tok_rows, head_count, nope_width + rope_width)
    q_latent = jnp.einsum(
        "thn,hnc->thc", q_split[:, :, :nope_width], uk_weight, preferred_element_type=jnp.float32
    ).astype(jnp.bfloat16)
    q_abs = jnp.concatenate([q_latent, q_split[:, :, nope_width:]], axis=2)
    x_count = lax.axis_size("x")
    z_count = lax.axis_size("z")
    suffix_rows = lax.all_gather(suffix_latent, ("y", "core"), axis=0, tiled=True)
    dest_slots = lax.all_to_all(
        jnp.broadcast_to(my_slot[None], (z_count,)), "z", 0, 0, tiled=True
    )
    x_chunks = lax.all_to_all(
        jnp.broadcast_to(prefix_latent[None], (x_count,) + prefix_latent.shape), "x", 0, 0, tiled=True
    )
    sent = jnp.take(x_chunks, dest_slots % x_count, axis=0)
    recv_chunks = lax.all_to_all(sent, "z", 0, 0, tiled=True)
    my_chunk = lax.dynamic_index_in_dim(recv_chunks, my_slot // x_count, 0, keepdims=False)
    prefix_rows = lax.all_gather(my_chunk, ("y", "core"), axis=0, tiled=True)
    key_rows = jnp.concatenate([prefix_rows, suffix_rows], axis=0)
    key_pos = jnp.arange(suffix_rows.shape[0], dtype=jnp.int32)
    key_request = request_of(key_pos, lengths)
    visible_suffix = (key_request[None, :] == own_request[:, None]) & (
        key_pos[None, :] <= positions[:, None]
    )
    visible = jnp.concatenate(
        [jnp.ones((tok_rows, prefix_rows.shape[0]), jnp.bool_), visible_suffix], axis=1
    )
    scores = (
        jnp.einsum("thc,nc->thn", q_abs, key_rows, preferred_element_type=jnp.float32)
        * score_scale
    )
    scores = jnp.where(visible[:, None, :], scores, masked_score)
    top_score = jnp.max(scores, axis=2, keepdims=True)
    prob_terms = jnp.where(visible[:, None, :], jnp.exp(scores - top_score), 0.0)
    weight_sum = jnp.sum(prob_terms, axis=2)
    latent_acc = jnp.einsum(
        "thn,nc->thc",
        prob_terms.astype(jnp.bfloat16),
        key_rows[:, :kv_rank],
        preferred_element_type=jnp.float32,
    )
    latent_out = (latent_acc / weight_sum[:, :, None]).astype(jnp.bfloat16)
    heads_out = jnp.einsum(
        "thc,hcv->thv", latent_out, uv_weight, preferred_element_type=jnp.float32
    ).astype(jnp.bfloat16)
    heads_out = heads_out.reshape(tok_rows, -1)
    attended = jnp.dot(heads_out, out_weight, preferred_element_type=jnp.float32).astype(
        jnp.bfloat16
    )
    residual = hidden.astype(jnp.float32) + attended.astype(jnp.float32)
    mean_square = jnp.mean(residual * residual, axis=1, keepdims=True)
    normed = (residual * lax.rsqrt(mean_square + 1e-06) * norm_gain).astype(jnp.bfloat16)
    experts = EXPERTS
    capacity = -(-CAP // 16) * 16
    top_picks = expert_ids.shape[1]
    slots = experts * capacity
    flat_ids = expert_ids.reshape(-1)
    onehot = (flat_ids[:, None] == jnp.arange(experts, dtype=jnp.int32)[None, :]).astype(jnp.int32)
    slot_rank = jnp.sum((jnp.cumsum(onehot, axis=0) - 1) * onehot, axis=1)
    target = flat_ids * capacity + slot_rank
    hits = jnp.arange(slots, dtype=jnp.int32)[None, :] == target[:, None]
    placing = hits.astype(jnp.bfloat16).reshape(tok_rows, top_picks, slots).sum(axis=1)
    packed = lax.dot_general(
        placing, normed, (((0,), (0,)), ((), ())), preferred_element_type=jnp.float32
    ).astype(jnp.bfloat16)
    swap = [(0, 1), (1, 0)]
    sibling_gate = lax.ppermute(expert_gate, "core", swap)
    sibling_up = lax.ppermute(expert_up, "core", swap)
    sibling_down = lax.ppermute(expert_down, "core", swap)
    recv_rows = lax.all_to_all(packed, ("z", "x", "y"), 0, 0, tiled=True)

    def half_expert(gate_w, up_w, down_w):
        gate_proj = jnp.dot(recv_rows, gate_w, preferred_element_type=jnp.float32)
        up_proj = jnp.dot(recv_rows, up_w, preferred_element_type=jnp.float32)
        active = lax.optimization_barrier((jax.nn.silu(gate_proj) * up_proj).astype(jnp.bfloat16))
        return jnp.dot(active, down_w, preferred_element_type=jnp.float32).astype(jnp.bfloat16)

    own_part = half_expert(expert_gate[0], expert_up[0], expert_down[0])
    sibling_part = half_expert(sibling_gate[0], sibling_up[0], sibling_down[0])
    pair_total = (own_part.astype(jnp.float32) + sibling_part.astype(jnp.float32)).astype(
        jnp.bfloat16
    )
    returned = lax.all_to_all(pair_total, ("z", "x", "y"), 0, 0, tiled=True)
    pick_weight = jnp.sum(
        jnp.where(hits.reshape(tok_rows, top_picks, slots), gate_weights[:, :, None], 0.0), axis=1
    )
    weight_high = pick_weight.astype(jnp.bfloat16)
    weight_low = (pick_weight - weight_high.astype(jnp.float32)).astype(jnp.bfloat16)
    routed = jnp.dot(weight_high, returned, preferred_element_type=jnp.float32) + jnp.dot(
        weight_low, returned, preferred_element_type=jnp.float32
    )
    layer_out = (residual + routed).astype(jnp.bfloat16)
    return (attended, layer_out)


def solution(mesh):
    req_count = mesh.shape["req"]
    exp_count = mesh.shape["exp"]
    x_count = 4
    chip_mesh = Mesh(
        mesh.devices.reshape(req_count // x_count, x_count, exp_count // 2, 2),
        ("z", "x", "y", "core"),
    )
    rows = ("z", "x", "y", "core")
    groups = ("z", "x")
    in_specs = (
        P(rows, None),
        P(rows, None),
        P(rows, None),
        P(rows, None),
        P(),
        P(),
        P(),
        P(),
        P(rows, None, None),
        P(rows, None, None),
        P(rows, None, None),
        P(groups, None),
        P(groups, None),
        P(),
        P(rows, None),
        P(rows, None),
    )
    out_specs = (P(rows, None), P(rows, None))
    return jax.shard_map(
        layer, mesh=chip_mesh, in_specs=in_specs, out_specs=out_specs, check_vma=False
    )
```

```python
import jax
import jax.numpy as jnp
from jax import lax
from jax.sharding import Mesh, PartitionSpec as P

EXPERTS = 64
CAP = 14


masked_score = -1e30


def request_of(positions, lengths):
    request_ends = jnp.cumsum(lengths)
    return jnp.sum((positions[:, None] >= request_ends[None, :]).astype(jnp.int32), axis=1)


def layer(
    hidden,
    queries,
    suffix_latent,
    prefix_latent,
    uk_weight,
    uv_weight,
    out_weight,
    norm_gain,
    expert_gate,
    expert_up,
    expert_down,
    suffix_lengths,
    prefix_ids,
    prefix_owner,
    expert_ids,
    gate_weights,
):
    tok_rows = hidden.shape[0]
    head_count = uk_weight.shape[0]
    nope_width = uk_weight.shape[1]
    kv_rank = uk_weight.shape[2]
    rope_width = queries.shape[1] // head_count - nope_width
    score_scale = (nope_width + rope_width) ** (-0.5)
    column = lax.axis_index("y") * lax.axis_size("core") + lax.axis_index("core")
    positions = column * tok_rows + jnp.arange(tok_rows, dtype=jnp.int32)
    lengths = suffix_lengths[0]
    own_request = request_of(positions, lengths)
    my_slot = prefix_owner[prefix_ids[0, 0]]
    q_split = queries.reshape(tok_rows, head_count, nope_width + rope_width)
    q_latent = jnp.einsum(
        "thn,hnc->thc", q_split[:, :, :nope_width], uk_weight, preferred_element_type=jnp.float32
    ).astype(jnp.bfloat16)
    q_abs = jnp.concatenate([q_latent, q_split[:, :, nope_width:]], axis=2)
    x_count = lax.axis_size("x")
    z_count = lax.axis_size("z")
    suffix_rows = lax.all_gather(suffix_latent, ("y", "core"), axis=0, tiled=True)
    dest_slots = lax.all_to_all(
        jnp.broadcast_to(my_slot[None], (z_count,)), "z", 0, 0, tiled=True
    )
    x_chunks = lax.all_to_all(
        jnp.broadcast_to(prefix_latent[None], (x_count,) + prefix_latent.shape), "x", 0, 0, tiled=True
    )
    sent = jnp.take(x_chunks, dest_slots % x_count, axis=0)
    recv_chunks = lax.all_to_all(sent, "z", 0, 0, tiled=True)
    my_chunk = lax.dynamic_index_in_dim(recv_chunks, my_slot // x_count, 0, keepdims=False)
    exp_count = lax.axis_size("y") * lax.axis_size("core")
    prefix_rows = lax.all_to_all(
        jnp.broadcast_to(my_chunk[None], (exp_count,) + my_chunk.shape), ("y", "core"), 0, 0, tiled=True
    ).reshape(exp_count * my_chunk.shape[0], my_chunk.shape[1])
    key_rows = jnp.concatenate([prefix_rows, suffix_rows], axis=0)
    key_pos = jnp.arange(suffix_rows.shape[0], dtype=jnp.int32)
    key_request = request_of(key_pos, lengths)
    visible_suffix = (key_request[None, :] == own_request[:, None]) & (
        key_pos[None, :] <= positions[:, None]
    )
    visible = jnp.concatenate(
        [jnp.ones((tok_rows, prefix_rows.shape[0]), jnp.bool_), visible_suffix], axis=1
    )
    scores = (
        jnp.einsum("thc,nc->thn", q_abs, key_rows, preferred_element_type=jnp.float32)
        * score_scale
    )
    scores = jnp.where(visible[:, None, :], scores, masked_score)
    top_score = jnp.max(scores, axis=2, keepdims=True)
    prob_terms = jnp.where(visible[:, None, :], jnp.exp(scores - top_score), 0.0)
    weight_sum = jnp.sum(prob_terms, axis=2)
    latent_acc = jnp.einsum(
        "thn,nc->thc",
        prob_terms.astype(jnp.bfloat16),
        key_rows[:, :kv_rank],
        preferred_element_type=jnp.float32,
    )
    latent_out = (latent_acc / weight_sum[:, :, None]).astype(jnp.bfloat16)
    heads_out = jnp.einsum(
        "thc,hcv->thv", latent_out, uv_weight, preferred_element_type=jnp.float32
    ).astype(jnp.bfloat16)
    heads_out = heads_out.reshape(tok_rows, -1)
    attended = jnp.dot(heads_out, out_weight, preferred_element_type=jnp.float32).astype(
        jnp.bfloat16
    )
    residual = hidden.astype(jnp.float32) + attended.astype(jnp.float32)
    mean_square = jnp.mean(residual * residual, axis=1, keepdims=True)
    normed = (residual * lax.rsqrt(mean_square + 1e-06) * norm_gain).astype(jnp.bfloat16)
    experts = EXPERTS
    capacity = -(-CAP // 16) * 16
    top_picks = expert_ids.shape[1]
    slots = experts * capacity
    flat_ids = expert_ids.reshape(-1)
    onehot = (flat_ids[:, None] == jnp.arange(experts, dtype=jnp.int32)[None, :]).astype(jnp.int32)
    slot_rank = jnp.sum((jnp.cumsum(onehot, axis=0) - 1) * onehot, axis=1)
    target = flat_ids * capacity + slot_rank
    hits = jnp.arange(slots, dtype=jnp.int32)[None, :] == target[:, None]
    placing = hits.astype(jnp.bfloat16).reshape(tok_rows, top_picks, slots).sum(axis=1)
    packed = lax.dot_general(
        placing, normed, (((0,), (0,)), ((), ())), preferred_element_type=jnp.float32
    ).astype(jnp.bfloat16)
    swap = [(0, 1), (1, 0)]
    sibling_gate = lax.ppermute(expert_gate, "core", swap)
    sibling_up = lax.ppermute(expert_up, "core", swap)
    sibling_down = lax.ppermute(expert_down, "core", swap)
    recv_rows = lax.all_to_all(packed, ("z", "x", "y"), 0, 0, tiled=True)

    def half_expert(gate_w, up_w, down_w):
        gate_proj = jnp.dot(recv_rows, gate_w, preferred_element_type=jnp.float32)
        up_proj = jnp.dot(recv_rows, up_w, preferred_element_type=jnp.float32)
        active = lax.optimization_barrier((jax.nn.silu(gate_proj) * up_proj).astype(jnp.bfloat16))
        return jnp.dot(active, down_w, preferred_element_type=jnp.float32).astype(jnp.bfloat16)

    own_part = half_expert(expert_gate[0], expert_up[0], expert_down[0])
    sibling_part = half_expert(sibling_gate[0], sibling_up[0], sibling_down[0])
    pair_total = (own_part.astype(jnp.float32) + sibling_part.astype(jnp.float32)).astype(
        jnp.bfloat16
    )
    returned = lax.all_to_all(pair_total, ("z", "x", "y"), 0, 0, tiled=True)
    pick_weight = jnp.sum(
        jnp.where(hits.reshape(tok_rows, top_picks, slots), gate_weights[:, :, None], 0.0), axis=1
    )
    routed = jnp.dot(
        pick_weight,
        returned.astype(jnp.float32),
        precision=lax.Precision.HIGHEST,
        preferred_element_type=jnp.float32,
    )
    layer_out = (residual + routed).astype(jnp.bfloat16)
    return (attended, layer_out)


def solution(mesh):
    req_count = mesh.shape["req"]
    exp_count = mesh.shape["exp"]
    x_count = 4
    chip_mesh = Mesh(
        mesh.devices.reshape(req_count // x_count, x_count, exp_count // 2, 2),
        ("z", "x", "y", "core"),
    )
    rows = ("z", "x", "y", "core")
    groups = ("z", "x")
    in_specs = (
        P(rows, None),
        P(rows, None),
        P(rows, None),
        P(rows, None),
        P(),
        P(),
        P(),
        P(),
        P(rows, None, None),
        P(rows, None, None),
        P(rows, None, None),
        P(groups, None),
        P(groups, None),
        P(),
        P(rows, None),
        P(rows, None),
    )
    out_specs = (P(rows, None), P(rows, None))
    return jax.shard_map(
        layer, mesh=chip_mesh, in_specs=in_specs, out_specs=out_specs, check_vma=False
    )
```
